32 devices in a mesh: seq: 4 (over y, core), shard: 8 (over z, x).
Axes of the slice: x: 2, y: 2, z: 4, core: 2. Of those that a mesh axis runs over, the one named last changes fastest.
Arguments:
- tokens: bfloat16 [16384, 768], P(('shard', 'seq')), may hold values from -6 to 6
- doc_lengths: int32 [32], replicated, may hold values from 1 to 1024, 16384 in all
- joint_weight: bfloat16 [768, 2304], P(('seq', 'shard')), may hold values from -0.21875 to 0.21875
- query_bias: bfloat16 [768], P(('seq', 'shard')), may hold values from -3 to 3
- value_bias: bfloat16 [768], P(('seq', 'shard')), may hold values from -3 to 3
- output_weight: bfloat16 [768, 768], P(('seq', 'shard')), may hold values from -1.75 to 1.75
- output_bias: bfloat16 [768], P(('seq', 'shard')), may hold values from -3 to 3
- first_gain: bfloat16 [768], P(('seq', 'shard')), may hold values from 0.5 to 1.5
- first_shift: bfloat16 [768], P(('seq', 'shard')), may hold values from -3 to 3
- inner_weight: bfloat16 [768, 3072], P(('seq', 'shard')), may hold values from -0.21875 to 0.21875
- inner_bias: bfloat16 [3072], P(('seq', 'shard')), may hold values from -3 to 3
- outer_weight: bfloat16 [3072, 768], P(('seq', 'shard')), may hold values from -0.109375 to 0.109375
- outer_bias: bfloat16 [768], P(('seq', 'shard')), may hold values from -3 to 3
- second_gain: bfloat16 [768], P(('seq', 'shard')), may hold values from 0.5 to 1.5
- second_shift: bfloat16 [768], P(('seq', 'shard')), may hold values from -3 to 3
- cotangent: bfloat16 [16384, 768], P(('shard', 'seq')), may hold values from -6 to 6
Outputs:
- layer_out: bfloat16 [16384, 768], P(('shard', 'seq'))
- tokens_grad: float32 [16384, 768], P(('shard', 'seq'))
- joint_weight_grad: float32 [768, 2304], P(('seq', 'shard'))
- query_bias_grad: float32 [768], P(('seq', 'shard'))
- value_bias_grad: float32 [768], P(('seq', 'shard'))
- output_weight_grad: float32 [768, 768], P(('seq', 'shard'))
- output_bias_grad: float32 [768], P(('seq', 'shard'))
- first_gain_grad: float32 [768], P(('seq', 'shard'))
- first_shift_grad: float32 [768], P(('seq', 'shard'))
- inner_weight_grad: float32 [768, 3072], P(('seq', 'shard'))
- inner_bias_grad: float32 [3072], P(('seq', 'shard'))
- outer_weight_grad: float32 [3072, 768], P(('seq', 'shard'))
- outer_bias_grad: float32 [768], P(('seq', 'shard'))
- second_gain_grad: float32 [768], P(('seq', 'shard'))
- second_shift_grad: float32 [768], P(('seq', 'shard'))
The draws below stay inside these ranges and needn't reach their ends.
Inputs may be any that keep to these rules, and one draw needn't show every extreme that they name: `doc_lengths`: the documents fill the stream in order; running sums of the lengths before each document are its start offset; the longest has exactly 1024 tokens.
All inputs are finite; a program needn't handle non-finite values.
Results may differ from the reference program's by a relative error of at most 0.013.
The reference program's roundings to bfloat16 on the way count: a program that leaves them out, or rounds other values in their place, can miss the bound.
Values may be sent and summed in bfloat16 or wider, within the bound.
No kernel may reach another device: no remote copies, remote signals or barrier semaphores. Data moves between devices by JAX's collectives and lax.ppermute only.
A program may use at most 192 MiB of HBM per device.

```python
import math
import jax
import jax.numpy as jnp
import numpy as np
from jax import lax

D = 768
HEADS = 12
HEAD = 64
FF = 3072
TOK_DEV = 512
DOCMAX = 1024
TOKENS = 16384
NDOCS = 32
N_SEQ = 4


def strengthened(values, stream_key, source, target, shards_of, factor):
    def block_of(axis_at):
        return (jnp.arange(values.shape[axis_at]) // (values.shape[axis_at] // shards_of)).reshape((-1,) + (1,) * (values.ndim - 1 - axis_at))

    near = jax.random.permutation(stream_key, shards_of)[block_of(target)]
    far = (block_of(target) + shards_of // 2) % shards_of
    return jnp.where((block_of(source) == near) | (block_of(source) == far), factor * values, values)


def level_of(own_key, dims, pieces, least, high):
    loudness, own = 1.0, jax.random.fold_in(own_key, 6)
    for position, shards_of in pieces:
        draws = jnp.exp(jax.random.uniform(jax.random.fold_in(own, position), (shards_of,), jnp.float32, least / len(pieces), high / len(pieces)))
        loudness = loudness * jnp.repeat(draws, dims[position] // shards_of).reshape([-1 if axis == position else 1 for axis in range(len(dims))])
    return loudness


def length_profile(amount, total, reach, lean):
    weights = [(1 << 20) // math.isqrt(grade ** lean) + 1 for grade in range(2, amount + 1)]
    rest, holding = total - reach - (amount - 1), [1] * (amount - 1)
    while rest > 0:
        candidates = [i for i in range(amount - 1) if holding[i] < reach]
        whole, left = sum([weights[i] for i in candidates]), rest
        for i in candidates:
            extra = min(reach - holding[i], max(1, left * weights[i] // whole), rest)
            holding[i] = holding[i] + extra
            rest = rest - extra
    return np.array([reach] + holding)


def ragged_sizes(stream_key, count, total, reach, lean):
    if count == 2:
        one = jax.random.randint(stream_key, (), max(1, total - reach), min(reach, total - 1) + 1)
        return jnp.stack([one, total - one])
    tallies = jnp.asarray(length_profile(count, total, reach, lean), jnp.int32)
    twos = (count - 1) // 2
    giver, taker = tallies[1:1 + 2 * twos:2], tallies[2:2 + 2 * twos:2]
    margin = jnp.minimum(giver - 1, reach - taker)
    shifted = jax.random.randint(jax.random.fold_in(stream_key, 1), (twos,), 0, 1 << 20) % (margin + 1)
    tallies = tallies.at[1:1 + 2 * twos:2].set(giver - shifted).at[2:2 + 2 * twos:2].set(taker + shifted)
    return tallies[jax.random.permutation(jax.random.fold_in(stream_key, 2), count)]


def scatter_about(stream_key, dims, scale, bound, cuts=(), held_as=jnp.bfloat16):
    entries = scale * jax.random.normal(stream_key, dims, jnp.float32)
    if cuts:
        entries = entries * level_of(stream_key, dims, cuts, -0.22, 0.18)
    return jnp.clip(entries, -bound, bound).astype(held_as)


def bell_draw_with(rng, shape, scale, most, pieces, heavy, kind=jnp.bfloat16):
    values = scale * jax.random.normal(rng, shape, jnp.float32)
    if pieces:
        values = values * level_of(rng, shape, pieces, -0.22, 0.18)
    return jnp.clip(strengthened(values, jax.random.fold_in(rng, 3), *heavy), -most, most).astype(kind)


def setup_inputs(seed: int = 0) -> dict:
    streams_of = jax.random.split(jax.random.key(seed), 17)
    return {
        "tokens": bell_draw_with(streams_of[0], (TOKENS, D), 1.0, 6.0, ((0, 32),), (0, 1, 32, 2.75)),
        "doc_lengths": ragged_sizes(streams_of[1], NDOCS, TOKENS, DOCMAX, 2).astype(jnp.int32),
        "joint_weight": scatter_about(streams_of[2], (D, 3 * D), D ** -0.5, 0.21875, ((0, 32),)),
        "query_bias": scatter_about(streams_of[3], (D,), 0.5, 3.0, ((0, 32),)),
        "value_bias": scatter_about(streams_of[4], (D,), 0.5, 3.0, ((0, 32),)),
        "output_weight": scatter_about(streams_of[5], (D, D), (D // 64) ** -0.5, 1.75, ((0, 32),)),
        "output_bias": scatter_about(streams_of[6], (D,), 0.5, 3.0, ((0, 32),)),
        "first_gain": jnp.clip(1.0 + 0.1 * jax.random.normal(streams_of[7], (D,), jnp.float32), 0.5, 1.5).astype(jnp.bfloat16),
        "first_shift": scatter_about(streams_of[8], (D,), 0.5, 3.0, ((0, 32),)),
        "inner_weight": scatter_about(streams_of[9], (D, FF), D ** -0.5, 0.21875, ((0, 32),)),
        "inner_bias": scatter_about(streams_of[10], (FF,), 0.5, 3.0, ((0, 32),)),
        "outer_weight": scatter_about(streams_of[11], (FF, D), FF ** -0.5, 0.109375, ((0, 32),)),
        "outer_bias": scatter_about(streams_of[12], (D,), 0.5, 3.0, ((0, 32),)),
        "second_gain": jnp.clip(1.0 + 0.1 * jax.random.normal(streams_of[13], (D,), jnp.float32), 0.5, 1.5).astype(jnp.bfloat16),
        "second_shift": scatter_about(streams_of[14], (D,), 0.5, 3.0, ((0, 32),)),
        "cotangent": scatter_about(streams_of[15], (TOKENS, D), 1.0, 6.0, ((0, 32),)),
    }


@jax.custom_vjp
def low(v):
    return lax.optimization_barrier(v.astype(jnp.bfloat16)).astype(jnp.float32)

@jax.custom_vjp
def low_back(v):
    return v

def low_keep(v):
    return (low(v), None)

def low_pass(kept, grad):
    return (grad,)

def back_keep(v):
    return (v, None)

def back_low(kept, grad):
    return (low(grad),)
low.defvjp(low_keep, low_pass)
low_back.defvjp(back_keep, back_low)
epsilon = 1e-12
highest = lax.Precision.HIGHEST

def matmul(left, right):
    return jnp.dot(left, right, precision=highest, preferred_element_type=jnp.float32)

def normalize(value, gain, shift):
    mean = lax.optimization_barrier(jnp.mean(value, axis=-1, keepdims=True))
    centred = value - mean
    spread = lax.optimization_barrier(jnp.mean(centred * centred, axis=-1, keepdims=True))
    return centred * lax.rsqrt(spread + epsilon) * gain + shift

def doc_ids(doc_lengths, positions):
    ends = jnp.cumsum(doc_lengths).astype(jnp.int32)
    inside = (ends[None, :] <= positions[:, None]).astype(jnp.int32)
    return lax.optimization_barrier(jnp.sum(inside, axis=1)).astype(jnp.int32)

def attend(queries, keys, values, doc_lengths):
    width = min(512, TOK_DEV * N_SEQ)
    span = width + 2 * DOCMAX
    positions = jnp.arange(TOKENS, dtype=jnp.int32)
    docs = doc_ids(doc_lengths, positions)
    pad_keys = jnp.pad(keys, ((DOCMAX, DOCMAX), (0, 0), (0, 0)))
    pad_values = jnp.pad(values, ((DOCMAX, DOCMAX), (0, 0), (0, 0)))
    pad_docs = jnp.pad(docs, (DOCMAX, DOCMAX), constant_values=-1).astype(jnp.int32)

    def one_block(start):
        query_blk = lax.dynamic_slice_in_dim(queries, start, width, 0)
        key_blk = lax.dynamic_slice_in_dim(pad_keys, start, span, 0)
        value_blk = lax.dynamic_slice_in_dim(pad_values, start, span, 0)
        query_docs = lax.dynamic_slice_in_dim(docs, start, width, 0)
        key_docs = lax.dynamic_slice_in_dim(pad_docs, start, span, 0)
        mask = query_docs[:, None] == key_docs[None, :]
        scores = jnp.einsum('qhd,khd->hqk', query_blk, key_blk, precision=highest) * HEAD ** (-0.5)
        scores = low_back(scores)
        scores = jnp.where(mask[None], scores, -jnp.inf)
        top = lax.optimization_barrier(jnp.max(scores, axis=-1, keepdims=True))
        weights = jnp.exp(scores - top)
        probs = low(weights / lax.optimization_barrier(jnp.sum(weights, axis=-1, keepdims=True)))
        return jnp.einsum('hqk,khd->qhd', probs, value_blk, precision=highest)
    starts = jnp.arange(TOKENS // width, dtype=jnp.int32) * width
    blocks = lax.map(jax.checkpoint(one_block), starts)
    return blocks.reshape(TOKENS, HEADS, HEAD)

def forward(tokens, joint_weight, query_bias, value_bias, output_weight, output_bias, first_gain, first_shift, inner_weight, inner_bias, outer_weight, outer_bias, second_gain, second_shift, doc_lengths):
    zeros = jnp.zeros_like(query_bias)
    joint = matmul(tokens, joint_weight) + jnp.concatenate([query_bias, zeros, value_bias])
    joint = low(low_back(joint))
    split = joint.reshape(TOKENS, 3, HEADS, HEAD)
    context = attend(split[:, 0], split[:, 1], split[:, 2], doc_lengths)
    context = low(low_back(context.reshape(TOKENS, D)))
    attn = low_back(matmul(context, output_weight) + output_bias)
    hidden = normalize(tokens + attn, first_gain, first_shift)
    inner = low_back(matmul(low(hidden), inner_weight) + inner_bias)
    active = low(jax.nn.gelu(inner, approximate=True))
    outer = low_back(matmul(active, outer_weight) + outer_bias)
    return normalize(hidden + outer, second_gain, second_shift)

def reference(tokens, doc_lengths, joint_weight, query_bias, value_bias, output_weight, output_bias, first_gain, first_shift, inner_weight, inner_bias, outer_weight, outer_bias, second_gain, second_shift, cotangent):
    inputs = [a.astype(jnp.float32) for a in (tokens, joint_weight, query_bias, value_bias, output_weight, output_bias, first_gain, first_shift, inner_weight, inner_bias, outer_weight, outer_bias, second_gain, second_shift)]

    def closed(*values):
        return forward(*values, doc_lengths)
    result, pull = jax.vjp(closed, *inputs)
    grads = pull(cotangent.astype(jnp.float32))
    return (result.astype(jnp.bfloat16), grads[0], grads[1], grads[2], grads[3], grads[4], grads[5], grads[6], grads[7], grads[8], grads[9], grads[10], grads[11], grads[12], grads[13])
```

```python
import functools

import jax
import jax.numpy as jnp
from jax import lax
from jax.experimental import pallas as pl
from jax.experimental.pallas import tpu as pltpu
from jax.sharding import Mesh
from jax.sharding import PartitionSpec as P

D = 768
HEADS = 12
HEAD = 64
DOCMAX = 1024
GROUPS = 4
GROUP_HEADS = HEADS // GROUPS
WIDTH = GROUP_HEADS * HEAD
SPARE = 8
MASKED = -1e30
EPSILON = 1e-12

f32 = jnp.float32
bf16 = jnp.bfloat16

SWAP = [(0, 1), (1, 0)]
PLANE = ("x", "y")


def product(left, right, left_dim, right_dim):
    dims = (((left_dim,), (right_dim,)), ((), ()))
    return lax.dot_general(left, right, dims, preferred_element_type=f32)


def place_keys(core, own_ref, other_ref, halo_refs, keys_ref, sems, piece):
    pieces = own_ref.shape[1] // piece
    before, after, before_other, after_other = halo_refs
    mine = pl.multiple_of(core * piece, piece)
    theirs = pl.multiple_of((1 - core) * piece, piece)
    rows = pl.ds(WIDTH, 2 * WIDTH)
    plane = 2 * piece
    behind = plane * (pieces + 1)
    moves = []
    for index in range(pieces):
        source = pl.ds(index * piece, piece)
        start = plane * (index + 1)
        moves.append((own_ref.at[rows, source], start + mine))
        moves.append((other_ref.at[rows, source], start + theirs))
    moves.append((before, mine))
    moves.append((before_other, theirs))
    moves.append((after, behind + mine))
    moves.append((after_other, behind + theirs))
    copies = [
        pltpu.make_async_copy(
            source, keys_ref.at[:, pl.ds(pl.multiple_of(start, piece), piece)], sems.at[index]
        )
        for index, (source, start) in enumerate(moves)
    ]
    for copy in copies:
        copy.start()
    for copy in copies:
        copy.wait()


def doc_mask(key_docs, query_docs):
    width = query_docs.shape[1]
    parts = [key_docs == query_docs[:, c : c + 128] for c in range(0, width, 128)]
    return jnp.concatenate(parts, axis=1) if len(parts) > 1 else parts[0]


def attend_kernel(
    scalars,
    q_ref,
    own_ref,
    other_ref,
    before_ref,
    after_ref,
    before_other_ref,
    after_other_ref,
    qdoc_ref,
    kdoc_ref,
    ctx_ref,
    out_ref,
    lse_ref,
    keys_ref,
    sems,
    *,
    step,
    piece,
):
    index = pl.program_id(0)
    rows = q_ref.shape[1]

    @pl.when(index == 0)
    def _():
        halos = (before_ref, after_ref, before_other_ref, after_other_ref)
        place_keys(scalars[0], own_ref, other_ref, halos, keys_ref, sems, piece)

    first = scalars[1 + 2 * index]
    last = scalars[2 + 2 * index]
    scale = jnp.asarray(HEAD**-0.5, bf16)
    queries = [q_ref[h * HEAD : (h + 1) * HEAD, :] * scale for h in range(GROUP_HEADS)]
    query_docs = qdoc_ref[0:1, :]

    def body(block, carry):
        at = pl.ds(pl.multiple_of(block * step, step), step)
        mask = doc_mask(kdoc_ref[at, :], query_docs)
        result = []
        for h in range(GROUP_HEADS):
            top, total, acc = carry[h]
            keys = keys_ref[h * HEAD : (h + 1) * HEAD, at]
            values = keys_ref[WIDTH + h * HEAD : WIDTH + (h + 1) * HEAD, at]
            scores = jnp.where(mask, product(keys, queries[h], 0, 0), MASKED)
            higher = jnp.maximum(top, jnp.max(scores, axis=0, keepdims=True))
            weights = jnp.exp(scores - higher)
            fade = jnp.exp(top - higher)
            total = total * fade + jnp.sum(weights, axis=0, keepdims=True)
            acc = acc * fade + product(values, weights.astype(bf16), 1, 0)
            result.append((higher, total, acc))
        return tuple(result)

    start = tuple(
        (
            jnp.full((1, rows), MASKED, f32),
            jnp.zeros((1, rows), f32),
            jnp.zeros((HEAD, rows), f32),
        )
        for _ in range(GROUP_HEADS)
    )
    final = lax.fori_loop(first, last, body, start)
    for h in range(GROUP_HEADS):
        top, total, acc = final[h]
        context = acc / total
        ctx_ref[0, h * HEAD : (h + 1) * HEAD, :] = context.astype(bf16)
        out_ref[h * HEAD : (h + 1) * HEAD, :] = context
        lse_ref[h : h + 1, :] = top + jnp.log(total)


def attend_back_kernel(
    scalars,
    q_ref,
    own_ref,
    other_ref,
    before_ref,
    after_ref,
    before_other_ref,
    after_other_ref,
    qdoc_ref,
    kdoc_ref,
    out_ref,
    lse_ref,
    grad_ref,
    dq_ref,
    mine_ref,
    theirs_ref,
    rim_ref,
    keys_ref,
    sums_ref,
    sems,
    *,
    step,
    piece,
):
    index = pl.program_id(0)
    rows = q_ref.shape[1]
    core = scalars[0]

    @pl.when(index == 0)
    def _():
        halos = (before_ref, after_ref, before_other_ref, after_other_ref)
        place_keys(core, own_ref, other_ref, halos, keys_ref, sems, piece)
        sums_ref[...] = jnp.zeros_like(sums_ref)

    first = scalars[1 + 2 * index]
    last = scalars[2 + 2 * index]
    scale = jnp.asarray(HEAD**-0.5, bf16)
    heads = [slice(h * HEAD, (h + 1) * HEAD) for h in range(GROUP_HEADS)]
    later = [slice(WIDTH + h * HEAD, WIDTH + (h + 1) * HEAD) for h in range(GROUP_HEADS)]
    queries = [q_ref[r, :] * scale for r in heads]
    grads = [grad_ref[0, r, :] for r in heads]
    means = [
        jnp.sum(grads[h].astype(f32) * out_ref[r, :], axis=0, keepdims=True)
        for h, r in enumerate(heads)
    ]
    norms = [lse_ref[h : h + 1, :] for h in range(GROUP_HEADS)]
    query_docs = qdoc_ref[0:1, :]

    def body(block, carry):
        at = pl.ds(pl.multiple_of(block * step, step), step)
        mask = doc_mask(kdoc_ref[at, :], query_docs)
        result = []
        for h in range(GROUP_HEADS):
            keys = keys_ref[heads[h], at]
            values = keys_ref[later[h], at]
            scores = product(keys, queries[h], 0, 0)
            probs = jnp.where(mask, jnp.exp(scores - norms[h]), 0.0)
            grad_probs = product(values, grads[h], 0, 0)
            grad_scores = (probs * (grad_probs - means[h])).astype(bf16)
            sums_ref[later[h], at] += product(grads[h], probs.astype(bf16), 1, 1)
            sums_ref[heads[h], at] += product(queries[h], grad_scores, 1, 1)
            result.append(carry[h] + product(keys, grad_scores, 1, 0))
        return tuple(result)

    start = tuple(jnp.zeros((HEAD, rows), f32) for _ in range(GROUP_HEADS))
    final = lax.fori_loop(first, last, body, start)
    for h in range(GROUP_HEADS):
        dq_ref[0, heads[h], :] = (final[h] * (HEAD**-0.5)).astype(bf16)

    @pl.when(index == pl.num_programs(0) - 1)
    def _():
        pieces = mine_ref.shape[0]
        plane = 2 * piece
        mine = pl.multiple_of(core * piece, piece)
        theirs = pl.multiple_of((1 - core) * piece, piece)

        def stretch(start):
            return sums_ref[:, pl.ds(pl.multiple_of(start, piece), piece)]

        for p in range(pieces):
            mine_ref[p] = stretch(plane * (p + 1) + mine)
            theirs_ref[p] = stretch(plane * (p + 1) + theirs).astype(bf16)
        behind = plane * (pieces + 1)
        rim_ref[0] = stretch(mine)
        rim_ref[1] = stretch(behind + mine)
        theirs_ref[pieces] = stretch(theirs).astype(bf16)
        theirs_ref[pieces + 1] = stretch(behind + theirs).astype(bf16)


def key_specs(rows, span, piece):
    def query_block(height):
        return pl.BlockSpec((height, rows), lambda i, s: (0, i))

    anywhere = pl.BlockSpec(memory_space=pl.ANY)
    specs = [query_block(WIDTH)] + [anywhere] * 6
    specs += [query_block(8), pl.BlockSpec((span, 128), lambda i, s: (0, 0))]
    per_piece = piece // rows
    piece_block = pl.BlockSpec((1, WIDTH, rows), lambda i, s: (i // per_piece, 0, i % per_piece))
    return specs, query_block, piece_block


def attend(scalars, joint, others, halos, query_docs, key_docs, piece, rows, step):
    span = key_docs.shape[0]
    queries = joint.shape[1]
    specs, query_block, piece_block = key_specs(rows, span, piece)
    return pl.pallas_call(
        functools.partial(attend_kernel, step=step, piece=piece),
        out_shape=(
            jax.ShapeDtypeStruct((queries // piece, WIDTH, piece), bf16),
            jax.ShapeDtypeStruct((WIDTH, queries), f32),
            jax.ShapeDtypeStruct((8, queries), f32),
        ),
        grid_spec=pltpu.PrefetchScalarGridSpec(
            num_scalar_prefetch=1,
            grid=(queries // rows,),
            in_specs=specs,
            out_specs=[piece_block, query_block(WIDTH), query_block(8)],
            scratch_shapes=[
                pltpu.VMEM((2 * WIDTH, span), bf16),
                pltpu.SemaphoreType.DMA((2 * (queries // piece) + 4,)),
            ],
        ),
        compiler_params=pltpu.CompilerParams(vmem_limit_bytes=48 << 20),
        name="attend",
    )(scalars, joint, joint, others, *halos, query_docs, key_docs)


def attend_back(
    scalars, joint, others, halos, query_docs, key_docs, out, lse, grad, piece, rows, step
):
    span = key_docs.shape[0]
    queries = joint.shape[1]
    pieces = queries // piece
    specs, query_block, piece_block = key_specs(rows, span, piece)

    def whole(shape):
        return pl.BlockSpec(shape, lambda i, s: (0,) * len(shape))

    sizes = ((pieces, 2 * WIDTH, piece), (pieces + 2, 2 * WIDTH, piece), (2, 2 * WIDTH, piece))
    return pl.pallas_call(
        functools.partial(attend_back_kernel, step=step, piece=piece),
        out_shape=(
            jax.ShapeDtypeStruct((pieces, WIDTH, piece), bf16),
            jax.ShapeDtypeStruct(sizes[0], f32),
            jax.ShapeDtypeStruct(sizes[1], bf16),
            jax.ShapeDtypeStruct(sizes[2], f32),
        ),
        grid_spec=pltpu.PrefetchScalarGridSpec(
            num_scalar_prefetch=1,
            grid=(queries // rows,),
            in_specs=specs + [query_block(WIDTH), query_block(8), piece_block],
            out_specs=[piece_block] + [whole(size) for size in sizes],
            scratch_shapes=[
                pltpu.VMEM((2 * WIDTH, span), bf16),
                pltpu.VMEM((2 * WIDTH, span), f32),
                pltpu.SemaphoreType.DMA((2 * pieces + 4,)),
            ],
        ),
        compiler_params=pltpu.CompilerParams(vmem_limit_bytes=56 << 20),
        name="attend_back",
    )(scalars, joint, joint, others, *halos, query_docs, key_docs, out, lse, grad)


def normalize_keep(value, gain, shift):
    mean = jnp.mean(value, axis=-1, keepdims=True)
    centred = value - mean
    spread = jnp.mean(centred * centred, axis=-1, keepdims=True)
    scale = lax.rsqrt(spread + EPSILON)
    normed = centred * scale
    return (normed * gain + shift, normed, scale)


def normalize_back(grad, normed, scale, gain):
    grad_normed = grad * gain
    first = jnp.mean(grad_normed, axis=-1, keepdims=True)
    second = jnp.mean(grad_normed * normed, axis=-1, keepdims=True)
    result = scale * (grad_normed - first - normed * second)
    return (result, jnp.sum(grad * normed, axis=0), jnp.sum(grad, axis=0))


def activate(value):
    return jax.nn.gelu(value, approximate=True)


def plane_tokens(tokens, x, y):
    rows = tokens.shape[0]
    half = rows // 2
    a, b = tokens[:half], tokens[half:]
    a_y = lax.ppermute(a, "y", SWAP)
    b_x = lax.ppermute(b, "x", SWAP)
    a_two = lax.ppermute(jnp.concatenate([a, a_y]), "x", SWAP)
    b_two = lax.ppermute(jnp.concatenate([b, b_x]), "y", SWAP)
    mine = 2 * x + y
    gathered = jnp.zeros((4, 2, half, D), tokens.dtype)

    def put(gathered, part, piece, side):
        return lax.dynamic_update_slice(gathered, part[None, None], (piece, side, 0, 0))

    gathered = put(gathered, a, mine, 0)
    gathered = put(gathered, b, mine, 1)
    gathered = put(gathered, a_y, mine ^ 1, 0)
    gathered = put(gathered, b_x, mine ^ 2, 1)
    gathered = put(gathered, a_two[:half], mine ^ 2, 0)
    gathered = put(gathered, a_two[half:], mine ^ 3, 0)
    gathered = put(gathered, b_two[:half], mine ^ 1, 1)
    gathered = put(gathered, b_two[half:], mine ^ 3, 1)
    return gathered.reshape(4 * rows, D)


def group_weight(joint_weight, query_bias, value_bias, y, core, z, x, planes):
    rows = joint_weight.shape[0]
    parts = joint_weight.reshape(rows, 3, GROUPS, WIDTH).transpose(2, 0, 1, 3)
    parts = parts.reshape(GROUPS, rows, 3 * WIDTH)
    place = (2 * z + x) * rows
    zero = jnp.zeros((1, WIDTH), bf16)
    bias = jnp.concatenate(
        [
            lax.dynamic_update_slice(zero, query_bias[None], (0, place)),
            zero,
            lax.dynamic_update_slice(zero, value_bias[None], (0, place)),
        ],
        axis=1,
    )
    group = 2 * y + core
    chosen = jnp.arange(GROUPS)[:, None, None] == group
    bias = jnp.where(chosen, bias[None], jnp.zeros((), bf16))
    spare = jnp.zeros((GROUPS, SPARE - 1, 3 * WIDTH), bf16)
    parts = jnp.concatenate([parts, bias, spare], axis=1)
    message = parts.reshape(1, 2, 2, rows + SPARE, 3 * WIDTH)
    message = jnp.broadcast_to(message, (planes,) + message.shape[1:])
    message = message.reshape(4 * planes, rows + SPARE, 3 * WIDTH)
    mine = lax.all_to_all(message, ("z", "x", "y"), split_axis=0, concat_axis=0, tiled=True)
    theirs = lax.ppermute(mine, "core", SWAP)
    both = jnp.stack([jnp.where(core == 0, mine, theirs), jnp.where(core == 0, theirs, mine)])
    both = both.reshape(2, planes, 2, 2, rows + SPARE, 3 * WIDTH)
    weight = both[:, :, :, :, :rows].transpose(3, 0, 1, 2, 4, 5).reshape(D, 3 * WIDTH)
    bias = jnp.sum(both[:, :, :, :, rows].astype(f32), axis=(0, 1, 2, 3))
    return weight, bias


def by_core(value, axis, core):
    size = value.shape[axis] // 4
    shape = value.shape[:axis] + (2, 2, size) + value.shape[axis + 1 :]
    parts = value.reshape(shape)
    merged = value.shape[:axis] + (2 * size,) + value.shape[axis + 1 :]
    mine = lax.dynamic_index_in_dim(parts, core, axis + 1, keepdims=False).reshape(merged)
    theirs = lax.dynamic_index_in_dim(parts, 1 - core, axis + 1, keepdims=False).reshape(merged)
    return mine, theirs


def scatter_sum(mine, theirs, planes):
    other = lax.ppermute(theirs.astype(bf16), "core", SWAP)
    total = (mine.astype(f32) + other.astype(f32)).astype(bf16)
    rows, columns = total.shape[-2:]
    total = total.reshape(2, planes, 2, rows, columns).transpose(2, 0, 1, 3, 4)
    total = total.reshape(4, planes, rows, columns)
    total = lax.all_to_all(total, PLANE, split_axis=0, concat_axis=0, tiled=True)
    total = jnp.sum(total.astype(f32), axis=0).astype(bf16)
    total = lax.all_to_all(total, "z", split_axis=0, concat_axis=0, tiled=True)
    return jnp.sum(total.astype(f32), axis=0)


def body(
    tokens,
    doc_lengths,
    joint_weight,
    query_bias,
    value_bias,
    output_weight,
    output_bias,
    first_gain,
    first_shift,
    inner_weight,
    inner_bias,
    outer_weight,
    outer_bias,
    second_gain,
    second_shift,
    cotangent,
):
    y, core = lax.axis_index("y"), lax.axis_index("core")
    z, x = lax.axis_index("z"), lax.axis_index("x")
    planes = lax.axis_size("z")
    devices = 8 * planes
    piece = tokens.shape[0]
    queries = 4 * piece
    plane_size = 8 * piece
    span = plane_size + 2 * DOCMAX
    total = plane_size * planes
    share = joint_weight.shape[0]
    hidden_units = inner_weight.shape[1]
    chunks = hidden_units // D
    axes = ("y", "core", "z", "x")

    outer_part = outer_weight.reshape(chunks, share, D).transpose(1, 0, 2).reshape(share, -1)
    joint_part = joint_weight.reshape(share, 3, GROUPS, WIDTH).transpose(0, 2, 1, 3)
    joint_part = joint_part.reshape(share, 3 * D)
    vectors = jnp.stack(
        [output_bias, first_gain, first_shift, outer_bias, second_gain, second_shift], axis=1
    )
    vectors = jnp.concatenate([vectors, inner_bias.reshape(chunks, share).T], axis=1)
    vectors = jnp.pad(vectors, ((0, 0), (0, 128 - vectors.shape[1])))
    packed = jnp.concatenate(
        [output_weight, inner_weight, outer_part, joint_part, vectors], axis=1
    )
    full = lax.all_gather(packed, axes, axis=0, tiled=True)
    ends = [D, D + hidden_units, D + 2 * hidden_units, 4 * D + 2 * hidden_units]
    output_full = full[:, : ends[0]]
    inner_full = full[:, ends[0] : ends[1]]
    outer_full = full[:, ends[1] : ends[2]].reshape(devices, share, chunks, D)
    outer_full = outer_full.transpose(0, 2, 1, 3).reshape(hidden_units, D)
    joint_full = full[:, ends[2] : ends[3]]
    rows = full[:, ends[3] :].astype(f32).T
    obias, gain_one, shift_one, ubias, gain_two, shift_two = [rows[i] for i in range(6)]
    ibias = rows[6 : 6 + chunks].reshape(chunks, devices, share).transpose(1, 0, 2).reshape(-1)

    doc_ends = jnp.cumsum(doc_lengths).astype(jnp.int32)
    query_at = z * plane_size + jnp.arange(4, dtype=jnp.int32)[:, None] * (2 * piece)
    query_at = (query_at + core * piece + jnp.arange(piece, dtype=jnp.int32)).reshape(-1)
    key_origin = z * plane_size - DOCMAX
    key_at = key_origin + jnp.arange(span, dtype=jnp.int32)
    query_docs = jnp.sum((doc_ends[:, None] <= query_at[None, :]).astype(jnp.int32), axis=0)
    query_docs = jnp.broadcast_to(query_docs[None], (8, queries))
    key_docs = jnp.sum((doc_ends[None, :] <= key_at[:, None]).astype(jnp.int32), axis=1)
    key_docs = jnp.where((key_at >= 0) & (key_at < total), key_docs, -1)
    key_docs = jnp.broadcast_to(key_docs[:, None], (span, 128))

    def ranges(rows, step):
        heads = query_at[::rows]
        tails = query_at[rows - 1 :: rows]
        lows = jnp.max(jnp.where(doc_ends[None] <= heads[:, None], doc_ends[None], 0), axis=1)
        highs = jnp.min(jnp.where(doc_ends[None] > tails[:, None], doc_ends[None], total), axis=1)
        first = jnp.clip((lows - key_origin) // step, 0, span // step)
        last = jnp.clip((highs - key_origin + step - 1) // step, 0, span // step)
        flat = jnp.stack([first, last], axis=1).reshape(-1)
        return jnp.concatenate([core[None], flat]).astype(jnp.int32)

    sizes = (min(512, piece), 512)
    back_sizes = (min(256, piece), 512)
    scalars = ranges(*sizes)
    back_scalars = ranges(*back_sizes)

    plane = plane_tokens(tokens, x, y)
    weight, bias = group_weight(joint_weight, query_bias, value_bias, y, core, z, x, planes)
    joint = (product(weight, plane, 0, 1) + bias[:, None]).astype(bf16)
    others = lax.ppermute(joint, "core", SWAP)
    upward = [(i, i + 1) for i in range(planes - 1)]
    downward = [(i + 1, i) for i in range(planes - 1)]
    before = lax.ppermute(joint[WIDTH:, queries - piece :], "z", upward)
    after = lax.ppermute(joint[WIDTH:, :piece], "z", downward)
    before_other = lax.ppermute(before, "core", SWAP)
    after_other = lax.ppermute(after, "core", SWAP)
    halos = (before, after, before_other, after_other)
    context, out, lse = attend(
        scalars, joint, others, halos, query_docs, key_docs, piece, *sizes
    )
    context = lax.all_to_all(context, PLANE, split_axis=0, concat_axis=0, tiled=True)
    context = context.reshape(D, piece)

    attn = product(context, output_full, 0, 0) + obias
    hidden, normed_one, scale_one = normalize_keep(tokens.astype(f32) + attn, gain_one, shift_one)
    hidden_low = hidden.astype(bf16)
    inner = product(hidden_low, inner_full, 1, 0) + ibias
    active, active_back = jax.vjp(activate, inner)
    active_low = active.astype(bf16)
    outer = product(active_low, outer_full, 1, 0) + ubias
    result, normed_two, scale_two = normalize_keep(hidden + outer, gain_two, shift_two)
    layer_out = result.astype(bf16)
    grad_two, grad_gain_two, grad_shift_two = normalize_back(
        cotangent.astype(f32), normed_two, scale_two, gain_two
    )
    grad_outer = grad_two.astype(bf16)
    grad_ubias = jnp.sum(grad_outer.astype(f32), axis=0)
    grad_active = product(grad_outer, outer_full, 1, 1)
    grad_inner = active_back(grad_active)[0].astype(bf16)
    grad_ibias = jnp.sum(grad_inner.astype(f32), axis=0)
    grad_hidden = grad_two + product(grad_inner, inner_full, 1, 1)
    grad_one, grad_gain_one, grad_shift_one = normalize_back(
        grad_hidden, normed_one, scale_one, gain_one
    )
    grad_attn = grad_one.astype(bf16)
    grad_obias = jnp.sum(grad_attn.astype(f32), axis=0)
    grad_context = product(output_full, grad_attn, 1, 1).astype(bf16)
    grad_group = lax.all_to_all(
        grad_context.reshape(4, WIDTH, piece), PLANE, split_axis=0, concat_axis=0, tiled=True
    )

    def spread(pair, rows, columns):
        return [part.reshape(2, planes, 2, rows, columns) for part in pair]

    outer_pair = [
        product(part, grad_outer, 0, 0).astype(bf16) for part in by_core(active_low, 1, core)
    ]
    outer_grad = scatter_sum(*spread(outer_pair, chunks * share, D), planes)
    inner_pair = [
        product(part, grad_inner, 0, 0).astype(bf16) for part in by_core(hidden_low, 1, core)
    ]
    inner_grad = scatter_sum(*spread(inner_pair, share, hidden_units), planes)
    small = jnp.stack(
        [grad_obias, grad_gain_one, grad_shift_one, grad_ubias, grad_gain_two, grad_shift_two]
    )
    small = small.reshape(6, devices, share).transpose(1, 0, 2).reshape(devices, 6 * share)
    small = jnp.concatenate([small, grad_ibias.reshape(devices, chunks * share)], axis=1)
    small = jnp.pad(small, ((0, 0), (0, D - small.shape[1])))
    small = jnp.pad(small[:, None], ((0, 0), (0, SPARE - 1), (0, 0)))
    small_pair = by_core(small, 0, core)
    output_pair = [product(part, grad_attn, 1, 0) for part in by_core(context, 0, core)]
    output_pair = [
        jnp.concatenate([m, s.reshape(2, planes, 2, SPARE, D)], axis=3).astype(bf16)
        for m, s in zip(spread(output_pair, share, D), small_pair)
    ]
    output_sum = scatter_sum(*output_pair, planes)
    output_grad = output_sum[:share]
    flat = output_sum[share]
    vectors = [flat[i * share : (i + 1) * share] for i in range(6)]
    g_obias, g_gain_one, g_shift_one, g_ubias, g_gain_two, g_shift_two = vectors
    g_ibias = flat[6 * share : 6 * share + chunks * share]

    dq, mine, theirs, rims = attend_back(
        back_scalars,
        joint,
        others,
        halos,
        query_docs,
        key_docs,
        out,
        lse,
        grad_group,
        piece,
        *back_sizes,
    )
    other = lax.ppermute(theirs, "core", SWAP)
    rims = (rims + other[4:].astype(f32)).astype(bf16)
    from_after = lax.ppermute(rims[0], "z", downward)
    from_before = lax.ppermute(rims[1], "z", upward)
    owned = mine + other[:4].astype(f32)
    owned = owned.at[3].add(from_after.astype(f32)).at[0].add(from_before.astype(f32))
    grad_joint = jnp.concatenate([dq, owned.astype(bf16)], axis=1)

    grad_own = lax.all_to_all(grad_joint, PLANE, split_axis=0, concat_axis=0, tiled=True)
    tokens_grad = grad_one + product(grad_own.reshape(3 * D, piece), joint_full, 0, 1)
    bias_part = jnp.sum(grad_joint.astype(f32), axis=(0, 2))
    bias_rows = jnp.pad(bias_part[None], ((0, SPARE - 1), (0, 0)))
    bias_rows = jnp.broadcast_to(bias_rows, (2, planes, 2, SPARE, 3 * WIDTH))
    pair = []
    for part in by_core(plane, 1, core):
        part = part.reshape(4, piece, 2 * D // 4)
        dims = (((0, 1), (0, 2)), ((), ()))
        grad = lax.dot_general(part, grad_joint, dims, preferred_element_type=f32)
        grad = grad.reshape(2, planes, 2, share, 3 * WIDTH)
        pair.append(jnp.concatenate([grad, bias_rows], axis=3))
    other = lax.ppermute(pair[1].astype(bf16), "core", SWAP)
    summed = (pair[0] + other.astype(f32)).astype(bf16)
    summed = summed.transpose(1, 2, 0, 3, 4).reshape(4 * planes, share + SPARE, 3 * WIDTH)
    summed = lax.all_to_all(summed, ("z", "x", "y"), split_axis=0, concat_axis=0, tiled=True)
    summed = summed.reshape(planes, GROUPS, share + SPARE, 3, WIDTH).astype(f32)
    summed = jnp.sum(summed, axis=0)
    joint_grad = summed[:, :share].transpose(1, 2, 0, 3).reshape(share, 3 * D)
    bias_grad = lax.dynamic_index_in_dim(summed[:, share], 2 * y + core, 0, keepdims=False)
    bias_grad = lax.dynamic_slice_in_dim(bias_grad, (2 * z + x) * share, share, 1)

    return (
        layer_out,
        tokens_grad,
        joint_grad,
        bias_grad[0],
        bias_grad[2],
        output_grad,
        g_obias,
        g_gain_one,
        g_shift_one,
        inner_grad,
        g_ibias,
        outer_grad,
        g_ubias,
        g_gain_two,
        g_shift_two,
    )


def solution(mesh):
    planes = mesh.shape["shard"] // 2
    split = Mesh(mesh.devices.reshape(2, 2, planes, 2), ("y", "core", "z", "x"))
    stream = P(("z", "x", "y", "core"), None)
    matrix = P(("y", "core", "z", "x"), None)
    vector = P(("y", "core", "z", "x"))
    return jax.shard_map(
        body,
        mesh=split,
        in_specs=(stream, P(), matrix, vector, vector, matrix)
        + (vector,) * 3
        + (matrix, vector, matrix)
        + (vector,) * 3
        + (stream,),
        out_specs=(stream, stream, matrix, vector, vector, matrix)
        + (vector,) * 3
        + (matrix, vector, matrix)
        + (vector,) * 3,
        check_vma=False,
    )
```
